1024 devices in a mesh: ctx: 128 (over z, x, core), head: 8 (over y).
Axes of the slice: x: 4, y: 8, z: 16, core: 2. Of those that a mesh axis runs over, the one named last changes fastest.
Arguments:
- queries: bfloat16 [32768, 64, 128], P('ctx', 'head'), may hold values from -16 to 16
- keys: bfloat16 [32768, 8, 128], P(('ctx', 'head')), may hold values from -8 to 8
- values: bfloat16 [32768, 8, 128], P(('ctx', 'head')), may hold values from -6 to 6
- grad_out: bfloat16 [32768, 64, 128], P('ctx', 'head'), may hold values from -6 to 6
- lengths: int32 [128], replicated, may hold values from 1 to 768, 32768 in all
Outputs:
- attended: bfloat16 [32768, 64, 128], P('ctx', 'head')
- d_queries: bfloat16 [32768, 64, 128], P('ctx', 'head')
- d_keys: bfloat16 [32768, 8, 128], P(('ctx', 'head'))
- d_values: bfloat16 [32768, 8, 128], P(('ctx', 'head'))
The draws below stay inside these ranges and needn't reach their ends.
Inputs may be any that keep to these rules, and one draw needn't show every extreme that they name: `lengths`: the 128 documents fill the window; the longest has exactly 768 tokens.
All inputs are finite; a program needn't handle non-finite values.
Results may differ from the reference program's by a relative error of at most 0.0085.
Values may be sent and summed in bfloat16 or wider, within the bound.
A program may use at most 64 MiB of HBM per device.

```python
import math
import jax
import jax.numpy as jnp
import numpy as np
from jax import lax

D_HEAD = 128
Q_HEADS = 64
KV_HEADS = 8
TOK_DEV = 256
BACK = 3
TOKENS = 32768
MOST = 768
DOCS = 128
N_CTX = 128


def draw_queries(key, part):
    base_key = jax.random.fold_in(jax.random.fold_in(key, 17), 0)
    entries = jnp.clip(jax.random.normal(base_key, (TOKENS, Q_HEADS, D_HEAD), jnp.float32), -4.0, 4.0)
    return entries.astype(jnp.bfloat16)


def draw_keys(key, part):
    base_key = jax.random.fold_in(jax.random.fold_in(key, 23), 0)
    entries = jnp.clip(jax.random.normal(base_key, (TOKENS, KV_HEADS, D_HEAD), jnp.float32), -4.0, 4.0)
    return entries.astype(jnp.bfloat16)


def block_scale(own_key, extent, cuts, low, largest):
    level = 1.0
    for axis_at, parts in cuts:
        draws = jax.random.uniform(jax.random.fold_in(jax.random.fold_in(own_key, 6), axis_at), (parts,), jnp.float32, low / len(cuts), largest / len(cuts))
        level = level * jnp.repeat(jnp.exp(draws), extent[axis_at] // parts).reshape((-1,) + (1,) * (len(extent) - 1 - axis_at))
    return level


def split_up(number_of, total, most, lean):
    loads = [(1 << 20) // math.isqrt(rank ** lean) + 1 for rank in range(2, number_of + 1)]
    spare, holding = total - most - (number_of - 1), [1] * (number_of - 1)
    while spare > 0:
        movable = [i for i in range(number_of - 1) if holding[i] < most]
        whole, budget = sum([loads[i] for i in movable]), spare
        for i in movable:
            addition = min(most - holding[i], max(1, budget * loads[i] // whole), spare)
            holding[i] = holding[i] + addition
            spare = spare - addition
    return np.array([most] + holding)


def ragged(rng, number_of, total, reach, slope):
    if number_of == 2:
        one = jax.random.randint(rng, (), max(1, total - reach), min(reach, total - 1) + 1)
        return jnp.stack([one, total - one])
    sizes = jnp.asarray(split_up(number_of, total, reach, slope), jnp.int32)
    twos = (number_of - 1) // 2
    donor, receiver = sizes[1:1 + 2 * twos:2], sizes[2:2 + 2 * twos:2]
    slack = jnp.minimum(donor - 1, reach - receiver)
    moved = jax.random.randint(jax.random.fold_in(rng, 1), (twos,), 0, 1 << 20) % (slack + 1)
    sizes = sizes.at[1:1 + 2 * twos:2].set(donor - moved).at[2:2 + 2 * twos:2].set(receiver + moved)
    return sizes[jax.random.permutation(jax.random.fold_in(rng, 2), number_of)]


def scatter_about(rng, dims, scale, most, shards=(), kind=jnp.bfloat16):
    result = scale * jax.random.normal(rng, dims, jnp.float32)
    if shards:
        result = result * block_scale(rng, dims, shards, -0.22, 0.18)
    return jnp.clip(result, -most, most).astype(kind)


def setup_inputs(seed: int = 0) -> dict:
    streams_of = jax.random.split(jax.random.key(seed), 6)
    queries = draw_queries(jax.random.fold_in(streams_of[5], 71), 0)
    keys = draw_keys(jax.random.fold_in(streams_of[5], 71), 0)
    values = scatter_about(streams_of[2], (TOKENS, KV_HEADS, D_HEAD), 1.0, 6.0, ((0, 1024),))
    grad_out = scatter_about(streams_of[3], (TOKENS, Q_HEADS, D_HEAD), 1.0, 6.0, ((0, 128), (1, 8)))
    lengths = ragged(streams_of[4], DOCS, TOKENS, MOST, 2).astype(jnp.int32)
    return {"queries": queries, "keys": keys, "values": values, "grad_out": grad_out, "lengths": lengths}


def head_pass(query_rows, grad_rows, key_rows, value_rows, allowed):
    inv_root = query_rows.shape[-1] ** -0.5
    scores = jnp.dot(query_rows, key_rows.T, preferred_element_type=jnp.float32) * inv_root
    masked = jnp.where(allowed, scores, -jnp.inf)
    top_score = jnp.max(masked, axis=1, keepdims=True)
    log_total = top_score + jnp.log(jnp.sum(jnp.exp(masked - top_score), axis=1, keepdims=True))
    probs = jnp.exp(masked - log_total)
    probs_low = probs.astype(jnp.bfloat16)
    attended = jnp.dot(probs_low, value_rows, preferred_element_type=jnp.float32).astype(jnp.bfloat16)
    correction = jnp.sum(grad_rows.astype(jnp.float32) * attended.astype(jnp.float32), axis=1, keepdims=True)
    grad_probs = jnp.dot(grad_rows, value_rows.T, preferred_element_type=jnp.float32)
    grad_scores = (probs * (grad_probs - correction)).astype(jnp.bfloat16)
    grad_values = jnp.dot(probs_low.T, grad_rows, preferred_element_type=jnp.float32)
    grad_query = (jnp.dot(grad_scores, key_rows, preferred_element_type=jnp.float32) * inv_root).astype(jnp.bfloat16)
    grad_keys = jnp.dot(grad_scores.T, query_rows, preferred_element_type=jnp.float32) * inv_root
    return attended, grad_query, grad_keys, grad_values


def group_pass(query_group, grad_group, key_rows, value_rows, allowed):
    def one_head(head_inputs):
        return head_pass(head_inputs[0], head_inputs[1], key_rows, value_rows, allowed)

    attended, grad_query, grad_keys, grad_values = lax.map(
        one_head, (jnp.moveaxis(query_group, 1, 0), jnp.moveaxis(grad_group, 1, 0)))
    return (jnp.moveaxis(attended, 0, 1), jnp.moveaxis(grad_query, 0, 1),
            jnp.sum(grad_keys, axis=0), jnp.sum(grad_values, axis=0))


def attend(query_split, grad_split, key_span, value_span, allowed):
    results = [group_pass(query_split[:, group], grad_split[:, group], key_span[:, group], value_span[:, group], allowed)
               for group in range(query_split.shape[1])]
    return tuple(jnp.stack([member[slot_index] for member in results], axis=1) for slot_index in range(4))


def doc_start(starts, positions):
    return jnp.max(jnp.where(starts[None, :] <= positions[:, None], starts[None, :], 0), axis=1)


def reference(queries, keys, values, grad_out, lengths):
    kv_heads = keys.shape[1]
    head_dim = keys.shape[2]
    per_group = queries.shape[1] // kv_heads
    span_rows = (BACK + 1) * TOK_DEV
    starts = (jnp.cumsum(lengths) - lengths).astype(jnp.int32)
    leading = jnp.zeros((BACK * TOK_DEV, kv_heads, head_dim), keys.dtype)
    key_padded = jnp.concatenate([leading, keys], axis=0)
    value_padded = jnp.concatenate([leading, values], axis=0)

    def one_block(block_index):
        offset = (block_index * TOK_DEV).astype(jnp.int32)
        query_split = lax.dynamic_slice_in_dim(queries, offset, TOK_DEV, 0).reshape(TOK_DEV, kv_heads, per_group, head_dim)
        grad_split = lax.dynamic_slice_in_dim(grad_out, offset, TOK_DEV, 0).reshape(TOK_DEV, kv_heads, per_group, head_dim)
        key_span = lax.dynamic_slice_in_dim(key_padded, offset, span_rows, 0)
        value_span = lax.dynamic_slice_in_dim(value_padded, offset, span_rows, 0)
        query_pos = offset + jnp.arange(TOK_DEV, dtype=jnp.int32)
        key_pos = offset - BACK * TOK_DEV + jnp.arange(span_rows, dtype=jnp.int32)
        query_start = doc_start(starts, query_pos)
        allowed = (key_pos[None, :] >= query_start[:, None]) & (key_pos[None, :] <= query_pos[:, None])
        return attend(query_split, grad_split, key_span, value_span, allowed)

    attended, grad_query, grad_keys, grad_values = lax.map(one_block, jnp.arange(N_CTX, dtype=jnp.int32))
    key_parts = grad_keys.reshape(N_CTX, BACK + 1, TOK_DEV, kv_heads, head_dim)
    value_parts = grad_values.reshape(N_CTX, BACK + 1, TOK_DEV, kv_heads, head_dim)
    key_total = jnp.zeros((N_CTX + BACK, TOK_DEV, kv_heads, head_dim), jnp.float32)
    value_total = jnp.zeros((N_CTX + BACK, TOK_DEV, kv_heads, head_dim), jnp.float32)
    for slot_index in range(BACK + 1):
        key_total = key_total.at[slot_index:slot_index + N_CTX].add(key_parts[:, slot_index])
        value_total = value_total.at[slot_index:slot_index + N_CTX].add(value_parts[:, slot_index])
    d_keys = key_total[BACK:].reshape(TOKENS, kv_heads, head_dim).astype(jnp.bfloat16)
    d_values = value_total[BACK:].reshape(TOKENS, kv_heads, head_dim).astype(jnp.bfloat16)
    attended = attended.reshape(TOKENS, Q_HEADS, head_dim)
    d_queries = grad_query.reshape(TOKENS, Q_HEADS, head_dim)
    return attended, d_queries, d_keys, d_values
```

```python
import functools
import math

import jax
import jax.numpy as jnp
from jax import lax
from jax.experimental import pallas as pl
from jax.experimental.pallas import tpu as pltpu
from jax.sharding import PartitionSpec as P

BACK = 3
SPAN = BACK + 1
TILE = 256
FAR = -1e30
MESH = pl.DeviceIdType.MESH
F32 = jnp.float32
BF16 = jnp.bfloat16
NT = (((1,), (1,)), ((), ()))


def outward(n):
    order = [0]
    for step in range(1, n // 2 + 1):
        order.append(step)
        if n - step != step:
            order.append(n - step)
    return order


def places(n_ctx):
    ctx, head = lax.axis_index("ctx"), lax.axis_index("head")
    core = lax.rem(ctx, 2)

    def at(distance):
        return lax.rem(ctx + n_ctx + distance, n_ctx)

    return head, core, at, at(1 - 2 * core)


def greet(n_head, head, at):
    barrier = pltpu.get_barrier_semaphore()
    for off in range(1, n_head):
        pl.semaphore_signal(
            barrier, inc=1, device_id={"head": lax.rem(head + off, n_head)}, device_id_type=MESH
        )
    for distance in (1, -1, 2, -2):
        pl.semaphore_signal(barrier, inc=1, device_id={"ctx": at(distance)}, device_id_type=MESH)
    return barrier


def remote(src, dst, send, recv, device):
    return pltpu.make_async_remote_copy(
        src_ref=src,
        dst_ref=dst,
        send_sem=send,
        recv_sem=recv,
        device_id=device,
        device_id_type=MESH,
    )


def fused_kernel(
    n_ctx,
    n_head,
    q_hbm,
    k_hbm,
    v_hbm,
    do_hbm,
    len_hbm,
    o_ref,
    dq_ref,
    dk_ref,
    dv_ref,
    qx,
    do_all,
    raw,
    wide,
    len_ref,
    mine,
    span,
    keyx,
    vals,
    keyt,
    valt,
    scores,
    dprob,
    low,
    dsc,
    tops,
    share,
    fix,
    own,
    part,
    land,
    second,
    total,
    home,
    load,
    send,
    recv,
    back_send,
    back_recv,
):
    head, core, at, partner = places(n_ctx)
    shard = lax.axis_index("ctx")
    n_rows, head_dim = do_all.shape
    tok = keyx.shape[0] // SPAN
    per_group = n_rows // tok
    group_rows = tok // n_head
    docs = len_ref.shape[1]
    inv_root = head_dim ** (-0.5)
    expo = inv_root * math.log2(math.e)
    tiles = n_rows // TILE
    order = outward(n_head)
    sends = []

    def started(copy):
        copy.start()
        sends.append(copy)

    barrier = greet(n_head, head, at)
    k_load = pltpu.make_async_copy(k_hbm, raw.at[0], load.at[0])
    v_load = pltpu.make_async_copy(v_hbm, raw.at[1], load.at[1])
    q_load = pltpu.make_async_copy(q_hbm, qx.at[:, pl.ds(0, head_dim)], load.at[2])
    do_load = pltpu.make_async_copy(do_hbm, do_all, load.at[3])
    len_load = pltpu.make_async_copy(len_hbm, len_ref, load.at[4])
    for copy in (k_load, v_load, len_load, q_load, do_load):
        copy.start()
    k_load.wait()
    v_load.wait()
    for which in range(2):
        wide[which] = raw[which].astype(F32)
    for j in range(n_head):
        for which in range(2):
            mine[j, which] = wide[which, pl.ds(j, group_rows, stride=n_head), :].astype(BF16)
    pl.semaphore_wait(barrier, n_head + 3)

    for off in reversed(order[1:]):
        to = lax.rem(head + off, n_head)
        started(
            remote(mine.at[to], span.at[0, head], send.at[0, off], recv.at[0, head], {"head": to})
        )
    started(remote(mine.at[head], span.at[2, head], send.at[2, 0], recv.at[2, head], {"ctx": at(2)}))
    span[0, head] = mine[head]

    len_load.wait()
    counts = len_ref[...].astype(F32)
    row_id = lax.broadcasted_iota(jnp.int32, (docs, docs), 0)
    lane_id = lax.broadcasted_iota(jnp.int32, (docs, docs), 1)
    column = jnp.sum(jnp.where(row_id == lane_id, counts, 0.0), axis=1, keepdims=True)
    ends = jnp.sum(jnp.where(row_id <= lane_id, column, 0.0), axis=0, keepdims=True).astype(jnp.int32)
    starts = ends - len_ref[...]
    for block in range(SPAN):
        pos = (shard - BACK + block) * tok + lax.broadcasted_iota(jnp.int32, (tok, docs), 0)
        inside = (pos >= starts) & (pos < ends)
        keyx[pl.ds(block * tok, tok), pl.ds(head_dim, docs)] = jnp.where(inside, 0.0, FAR).astype(BF16)

    def query_documents(i, carry):
        at_row = pl.ds(pl.multiple_of(i * TILE, TILE), TILE)
        q_tok = i * (TILE // per_group) + lax.broadcasted_iota(jnp.int32, (TILE, docs), 0) // per_group
        pos = shard * tok + q_tok
        inside = (pos >= starts) & (pos < ends)
        qx[at_row, pl.ds(head_dim, docs)] = jnp.where(inside, 1.0, 0.0).astype(BF16)
        return carry

    lax.fori_loop(0, tiles, query_documents, 0)

    for off in order[1:]:
        group = lax.rem(head + off, n_head)
        remote(
            mine.at[0], span.at[0, group], send.at[0, off], recv.at[0, group], {"head": group}
        ).wait_recv()
        started(
            remote(
                span.at[0, group], span.at[2, group], send.at[2, off], recv.at[2, group], {"ctx": at(2)}
            )
        )
    q_load.wait()
    do_load.wait()

    def rows_of(back):
        return pl.ds((BACK - back) * tok, tok)

    def lanes_of(i):
        return pl.ds(pl.multiple_of(i * TILE, TILE), TILE)

    def score_block(back):
        rows = rows_of(back)
        key_rows = span[back, :, 0].reshape(tok, head_dim)
        value_rows = span[back, :, 1].reshape(tok, head_dim)
        keyx[rows, pl.ds(0, head_dim)] = key_rows
        vals[rows, :] = value_rows
        keyt[:, rows] = key_rows.astype(F32).T.astype(BF16)
        valt[:, rows] = value_rows.astype(F32).T.astype(BF16)

        def step(i, carry):
            at_row = lanes_of(i)
            s = lax.dot_general(keyx[rows, :], qx[at_row, :], NT, preferred_element_type=F32)
            if back == 0:
                k_tok = lax.broadcasted_iota(jnp.int32, (tok, TILE), 0)
                r_tok = (
                    i * (TILE // per_group)
                    + lax.broadcasted_iota(jnp.int32, (tok, TILE), 1) // per_group
                )
                s = jnp.where(k_tok <= r_tok, s, FAR)
            scores[rows, at_row] = s
            tops[back : back + 1, at_row] = jnp.max(s, axis=0, keepdims=True)
            dprob[rows, at_row] = lax.dot_general(
                vals[rows, :], do_all[at_row, :], NT, preferred_element_type=F32
            )
            return carry

        lax.fori_loop(0, tiles, step, 0)

    score_block(0)
    for off in order:
        group = lax.rem(head + off, n_head)
        remote(
            span.at[0, group], span.at[2, group], send.at[2, off], recv.at[2, group], {"ctx": at(2)}
        ).wait_recv()
        started(
            remote(
                span.at[2, group], span.at[3, group], send.at[3, off], recv.at[3, group], {"ctx": at(1)}
            )
        )
        started(
            remote(
                span.at[2 * core, group],
                span.at[1, group],
                send.at[1, off],
                recv.at[1, group],
                {"ctx": partner},
            )
        )
    score_block(2)
    for slot, to in ((1, partner), (3, at(1))):
        for off in order:
            group = lax.rem(head + off, n_head)
            remote(
                span.at[2, group], span.at[slot, group], send.at[slot, off], recv.at[slot, group], {"ctx": to}
            ).wait_recv()
        score_block(slot)

    def normalise(i, carry):
        at_row = lanes_of(i)
        top = jnp.max(tops[0:SPAN, at_row], axis=0, keepdims=True) * expo
        mass = jnp.zeros_like(top)
        moment = jnp.zeros_like(top)
        for back in range(SPAN):
            rows = rows_of(back)
            e = jnp.exp2(scores[rows, at_row] * expo - top)
            scores[rows, at_row] = e
            mass = mass + jnp.sum(e, axis=0, keepdims=True)
            moment = moment + jnp.sum(e * dprob[rows, at_row], axis=0, keepdims=True)
        inverse = 1.0 / mass
        share[:, at_row] = inverse
        fix[:, at_row] = moment * inverse
        return carry

    lax.fori_loop(0, tiles, normalise, 0)

    def gradient_block(back):
        rows = rows_of(back)

        def step(i, carry):
            at_row = lanes_of(i)
            p = scores[rows, at_row] * share[:, at_row]
            low[rows, at_row] = p.astype(BF16)
            dsc[rows, at_row] = (p * (dprob[rows, at_row] - fix[:, at_row])).astype(BF16)
            return carry

        lax.fori_loop(0, tiles, step, 0)
        d_k = jnp.dot(dsc[rows, :], qx[:, pl.ds(0, head_dim)], preferred_element_type=F32) * inv_root
        d_v = jnp.dot(low[rows, :], do_all[...], preferred_element_type=F32)
        shape = (n_head, group_rows, head_dim)
        return d_k.reshape(shape), d_v.reshape(shape)

    def settle(back):
        for which, term in enumerate(gradient_block(back)):
            part[back - 1, :, which] = term.astype(BF16)

    for back, slot, to in ((3, 2, at(-1)), (1, 0, partner)):
        settle(back)
        started(remote(part.at[slot], land.at[slot], back_send.at[slot, 0], back_recv.at[slot, 0], {"ctx": to}))
    settle(2)
    for slot, to in ((2, at(-1)), (0, partner)):
        remote(
            part.at[slot], land.at[slot], back_send.at[slot, 0], back_recv.at[slot, 0], {"ctx": to}
        ).wait_recv()
    on_second = (core == 1).astype(F32)
    home_order = order[::-1]
    for off in home_order:
        group = lax.rem(head + off, n_head)
        term = part[1, group].astype(F32) + land[2, group].astype(F32)
        second[group] = (term + on_second * land[0, group].astype(F32)).astype(BF16)
        started(
            remote(
                second.at[group], land.at[1, group], back_send.at[1, off], back_recv.at[1, group], {"ctx": at(-2)}
            )
        )
    for which, term in enumerate(gradient_block(0)):
        own[:, which] = term

    def attended(i, carry):
        at_row = lanes_of(i)
        out = jnp.dot(valt[...], low[:, at_row], preferred_element_type=F32)
        o_ref[at_row, :] = out.T.astype(BF16)
        return carry

    lax.fori_loop(0, tiles, attended, 0)
    for off in home_order:
        group = lax.rem(head + off, n_head)
        remote(
            second.at[group], land.at[1, group], back_send.at[1, off], back_recv.at[1, group], {"ctx": at(-2)}
        ).wait_recv()
        term = own[group] + land[1, group].astype(F32)
        term = (term + (1.0 - on_second) * land[0, group].astype(F32)).astype(BF16)
        if off:
            total[group] = term
            started(
                remote(
                    total.at[group], home.at[head], back_send.at[3, off], back_recv.at[3, head], {"head": group}
                )
            )
        else:
            home[group] = term

    def d_queries(i, carry):
        at_row = lanes_of(i)
        out = jnp.dot(keyt[...], dsc[:, at_row], preferred_element_type=F32) * inv_root
        dq_ref[at_row, :] = out.T.astype(BF16)
        return carry

    lax.fori_loop(0, tiles, d_queries, 0)
    for off in home_order[:-1]:
        group = lax.rem(head + off, n_head)
        remote(
            total.at[group], home.at[group], back_send.at[3, off], back_recv.at[3, group], {"head": group}
        ).wait_recv()
    for j in range(n_head):
        for which in range(2):
            wide[which, pl.ds(j, group_rows, stride=n_head), :] = home[j, which].astype(F32)
    dk_ref[...] = wide[0].astype(BF16)
    dv_ref[...] = wide[1].astype(BF16)
    for copy in sends:
        copy.wait_send()


def store_kernel(*refs):
    count = (len(refs) - 1) // 2
    copies = [
        pltpu.make_async_copy(refs[i], refs[count + i], refs[-1].at[i]) for i in range(count)
    ]
    for copy in copies:
        copy.start()
    for copy in copies:
        copy.wait()


def on_device(n_ctx, n_head, queries, keys, values, grad_out, lengths):
    tok, per_group, head_dim = queries.shape
    group = keys.shape[0]
    rows = tok * per_group
    docs = lengths.shape[0]
    vmem = pl.BlockSpec(memory_space=pltpu.VMEM)
    far = pl.BlockSpec(memory_space=pltpu.HBM)
    share = (n_head, 2, group, head_dim)
    dma = pltpu.SemaphoreType.DMA
    results = (jax.ShapeDtypeStruct((rows, head_dim), BF16),) * 2 + (
        jax.ShapeDtypeStruct((group * n_head, head_dim), BF16),
    ) * 2
    kept = pl.pallas_call(
        functools.partial(fused_kernel, n_ctx, n_head),
        out_shape=results,
        in_specs=[far] * 5,
        out_specs=(vmem,) * 4,
        scratch_shapes=[
            pltpu.VMEM((rows, head_dim + docs), BF16),
            pltpu.VMEM((rows, head_dim), BF16),
            pltpu.VMEM((2, group * n_head, head_dim), BF16),
            pltpu.VMEM((2, group * n_head, head_dim), F32),
            pltpu.VMEM((1, docs), jnp.int32),
            pltpu.VMEM(share, BF16),
            pltpu.VMEM((SPAN,) + share, BF16),
            pltpu.VMEM((SPAN * tok, head_dim + docs), BF16),
            pltpu.VMEM((SPAN * tok, head_dim), BF16),
            pltpu.VMEM((head_dim, SPAN * tok), BF16),
            pltpu.VMEM((head_dim, SPAN * tok), BF16),
            pltpu.VMEM((SPAN * tok, rows), F32),
            pltpu.VMEM((SPAN * tok, rows), F32),
            pltpu.VMEM((SPAN * tok, rows), BF16),
            pltpu.VMEM((SPAN * tok, rows), BF16),
            pltpu.VMEM((8, rows), F32),
            pltpu.VMEM((1, rows), F32),
            pltpu.VMEM((1, rows), F32),
            pltpu.VMEM(share, F32),
            pltpu.VMEM((BACK,) + share, BF16),
            pltpu.VMEM((BACK,) + share, BF16),
            pltpu.VMEM(share, BF16),
            pltpu.VMEM(share, BF16),
            pltpu.VMEM(share, BF16),
            dma((5,)),
            dma((4, n_head)),
            dma((4, n_head)),
            dma((4, n_head)),
            dma((4, n_head)),
        ],
        compiler_params=pltpu.CompilerParams(
            collective_id=0, has_side_effects=True, vmem_limit_bytes=48 << 20
        ),
    )(
        *(
            pltpu.with_memory_space_constraint(x, pltpu.HBM)
            for x in (
                queries.reshape(rows, head_dim),
                keys.reshape(-1, head_dim),
                values.reshape(-1, head_dim),
                grad_out.reshape(rows, head_dim),
                lengths.reshape(1, -1),
            )
        )
    )
    attended, d_queries, d_keys, d_values = pl.pallas_call(
        store_kernel,
        out_shape=results,
        in_specs=[vmem] * 4,
        out_specs=(far,) * 4,
        scratch_shapes=[dma((4,))],
        compiler_params=pltpu.CompilerParams(vmem_limit_bytes=4 << 20),
    )(*kept)
    return (
        attended.reshape(queries.shape),
        d_queries.reshape(queries.shape),
        d_keys.reshape(keys.shape),
        d_values.reshape(values.shape),
    )


def solution(mesh):
    rows, groups = P("ctx", "head", None), P(("ctx", "head"), None, None)
    return jax.shard_map(
        functools.partial(on_device, mesh.shape["ctx"], mesh.shape["head"]),
        mesh=mesh,
        in_specs=(rows, groups, groups, rows, P()),
        out_specs=(rows, rows, groups, groups),
        check_vma=False,
    )
```

```python
import functools
import math

import jax
import jax.numpy as jnp
from jax import lax
from jax.experimental import pallas as pl
from jax.experimental.pallas import tpu as pltpu
from jax.sharding import PartitionSpec as P

BACK = 3
SPAN = BACK + 1
LAG = 3
UNROLL = 8
TILE = 256
FAR = -1e30
MESH = pl.DeviceIdType.MESH
F32 = jnp.float32
BF16 = jnp.bfloat16
NT = (((1,), (1,)), ((), ()))


def outward(n):
    order = [0]
    for step in range(1, n // 2 + 1):
        order.append(step)
        if n - step != step:
            order.append(n - step)
    return order


def places(n_ctx):
    ctx, head = lax.axis_index("ctx"), lax.axis_index("head")
    core = lax.rem(ctx, 2)

    def at(distance):
        return jnp.clip(ctx + distance, 0, n_ctx - 1)

    return head, core, at, ctx + 1 - 2 * core


def is_first(ctx, head):
    return (ctx == 0) & (head == 0)


def greet(n_ctx, n_head, head, shard):
    barrier = pltpu.get_barrier_semaphore()
    count = jnp.int32(0)
    greets = jnp.logical_not(is_first(shard, head))
    for off in range(1, n_head):
        to = lax.rem(head + off, n_head)

        @pl.when(greets)
        def _():
            pl.semaphore_signal(barrier, inc=1, device_id={"head": to}, device_id_type=MESH)

        count = count + jnp.logical_not(is_first(shard, to)).astype(jnp.int32)
    for distance in (1, -1, 2, -2):
        there = shard + distance
        exists = (there >= 0) & (there < n_ctx)

        @pl.when(exists & greets)
        def _():
            pl.semaphore_signal(barrier, inc=1, device_id={"ctx": there}, device_id_type=MESH)

        count = count + (exists & jnp.logical_not(is_first(there, head))).astype(jnp.int32)
    return barrier, count


def remote(src, dst, send, recv, device):
    return pltpu.make_async_remote_copy(
        src_ref=src,
        dst_ref=dst,
        send_sem=send,
        recv_sem=recv,
        device_id=device,
        device_id_type=MESH,
    )


def fused_kernel(
    n_ctx,
    n_head,
    q_hbm,
    k_hbm,
    v_hbm,
    do_hbm,
    len_hbm,
    o_ref,
    dq_ref,
    dk_ref,
    dv_ref,
    qx,
    do_all,
    raw,
    wide,
    len_ref,
    mine,
    span,
    keyx,
    vals,
    keyt,
    valt,
    scores,
    dprob,
    low,
    dsc,
    tops,
    share,
    fix,
    own,
    part,
    land,
    second,
    total,
    home,
    load,
    send,
    recv,
    back_send,
    back_recv,
    ready,
):
    head, core, at, partner = places(n_ctx)
    shard = lax.axis_index("ctx")
    n_rows, head_dim = do_all.shape
    tok = keyx.shape[0] // SPAN
    per_group = n_rows // tok
    group_rows = tok // n_head
    docs = len_ref.shape[1]
    inv_root = head_dim ** (-0.5)
    expo = inv_root * math.log2(math.e)
    tiles = n_rows // TILE
    order = outward(n_head)
    near = [lax.rem(head + off, n_head) for off in order]
    spot = sum(place * (group == 0).astype(jnp.int32) for place, group in enumerate(near))
    groups = [jnp.where(place < spot, near[place], near[place + 1]) for place in range(n_head - 1)]
    groups.append(jnp.int32(0))
    sends = []
    always = None

    def started(copy, when=always):
        if when is None:
            copy.start()
        else:
            pl.when(when)(copy.start)
        sends.append((copy, when))

    def awaited(copy, when=always):
        if when is None:
            copy.wait_recv()
        else:
            pl.when(when)(copy.wait_recv)

    back_one, back_two, back_three = shard >= 1, shard >= 2, shard >= 3
    on_one, on_two = shard + 1 < n_ctx, shard + 2 < n_ctx
    barrier, greeted = greet(n_ctx, n_head, head, shard)
    k_load = pltpu.make_async_copy(k_hbm, raw.at[0], load.at[0])
    v_load = pltpu.make_async_copy(v_hbm, raw.at[1], load.at[1])
    q_load = pltpu.make_async_copy(q_hbm, qx.at[:, pl.ds(0, head_dim)], load.at[2])
    do_load = pltpu.make_async_copy(do_hbm, do_all, load.at[3])
    len_load = pltpu.make_async_copy(len_hbm, len_ref, load.at[4])
    for copy in (k_load, v_load, len_load, q_load, do_load):
        copy.start()
    k_load.wait()
    v_load.wait()
    for which in range(2):
        wide[which] = raw[which].astype(F32)
    for j in range(n_head):
        for which in range(2):
            mine[j, which] = wide[which, pl.ds(j, group_rows, stride=n_head), :].astype(BF16)
    pl.semaphore_wait(barrier, greeted)

    @pl.when(is_first(shard, head))
    def _():
        for off in range(1, n_head):
            pl.semaphore_signal(
                ready, inc=1, device_id={"head": lax.rem(head + off, n_head)}, device_id_type=MESH
            )
        for distance in (1, 2):
            pl.semaphore_signal(ready, inc=1, device_id={"ctx": at(distance)}, device_id_type=MESH)


    for off in reversed(order[1:]):
        to = lax.rem(head + off, n_head)
        started(
            remote(mine.at[to], span.at[0, head], send.at[0, off], recv.at[0, head], {"head": to}),
            jnp.logical_not(is_first(shard, to)),
        )
    started(
        remote(mine.at[head], span.at[2, head], send.at[2, head], recv.at[2, head], {"ctx": at(2)}), on_two
    )
    span[0, head] = mine[head]
    for slot, there in ((1, back_one), (2, back_two), (3, back_three)):

        @pl.when(jnp.logical_not(there))
        def _():
            span[slot] = jnp.zeros(span.shape[1:], BF16)

    for slot, missing in (
        (0, (core == 1) & (shard < 2)),
        (1, shard + 2 >= n_ctx),
        (2, (shard + 1 >= n_ctx) | (shard < 2)),
    ):

        @pl.when(missing)
        def _():
            land[slot] = jnp.zeros(land.shape[1:], BF16)

    len_load.wait()
    counts = len_ref[...].astype(F32)
    row_id = lax.broadcasted_iota(jnp.int32, (docs, docs), 0)
    lane_id = lax.broadcasted_iota(jnp.int32, (docs, docs), 1)
    column = jnp.sum(jnp.where(row_id == lane_id, counts, 0.0), axis=1, keepdims=True)
    ends = jnp.sum(jnp.where(row_id <= lane_id, column, 0.0), axis=0, keepdims=True).astype(jnp.int32)
    starts = ends - len_ref[...]
    for block in range(SPAN):
        pos = (shard - BACK + block) * tok + lax.broadcasted_iota(jnp.int32, (tok, docs), 0)
        inside = (pos >= starts) & (pos < ends)
        keyx[pl.ds(block * tok, tok), pl.ds(head_dim, docs)] = jnp.where(inside, 0.0, FAR).astype(BF16)

    def query_documents(i, carry):
        at_row = pl.ds(pl.multiple_of(i * TILE, TILE), TILE)
        q_tok = i * (TILE // per_group) + lax.broadcasted_iota(jnp.int32, (TILE, docs), 0) // per_group
        pos = shard * tok + q_tok
        inside = (pos >= starts) & (pos < ends)
        qx[at_row, pl.ds(head_dim, docs)] = jnp.where(inside, 1.0, 0.0).astype(BF16)
        return carry

    lax.fori_loop(0, tiles, query_documents, 0)

    def relay(group):
        awaited(
            remote(
                span.at[0, group], span.at[2, group], send.at[2, group], recv.at[2, group], {"ctx": at(2)}
            ),
            back_two,
        )
        started(
            remote(
                span.at[2, group], span.at[3, group], send.at[3, group], recv.at[3, group], {"ctx": at(1)}
            ),
            back_two & on_one,
        )
        started(
            remote(
                span.at[2 * core, group],
                span.at[1, group],
                send.at[1, group],
                recv.at[1, group],
                {"ctx": partner},
            ),
            (core == 0) | back_two,
        )

    for place, group in enumerate(groups):
        other = group != head
        if place == n_head - 1:
            follows_first = (shard == 0) & (head > 0)

            @pl.when(follows_first)
            def _():
                pl.semaphore_wait(ready, 1)

            started(
                remote(
                    mine.at[0],
                    span.at[0, head],
                    send.at[0, lax.rem(n_head - head, n_head)],
                    recv.at[0, head],
                    {"head": 0},
                ),
                follows_first,
            )
        awaited(
            remote(mine.at[0], span.at[0, group], send.at[0, 0], recv.at[0, group], {"head": group}),
            other,
        )
        started(
            remote(
                span.at[0, group], span.at[2, group], send.at[2, group], recv.at[2, group], {"ctx": at(2)}
            ),
            on_two & other,
        )
        if place >= LAG:
            relay(groups[place - LAG])
    q_load.wait()
    do_load.wait()

    def rows_of(back):
        return pl.ds((BACK - back) * tok, tok)

    def lanes_of(i):
        return pl.ds(pl.multiple_of(i * TILE, TILE), TILE)

    def score_block(back):
        rows = rows_of(back)
        key_rows = span[back, :, 0].reshape(tok, head_dim)
        value_rows = span[back, :, 1].reshape(tok, head_dim)
        keyx[rows, pl.ds(0, head_dim)] = key_rows
        vals[rows, :] = value_rows
        keyt[:, rows] = key_rows.astype(F32).T.astype(BF16)
        valt[:, rows] = value_rows.astype(F32).T.astype(BF16)

        def step(i, carry):
            at_row = lanes_of(i)
            s = lax.dot_general(keyx[rows, :], qx[at_row, :], NT, preferred_element_type=F32) * expo
            if back == 0:
                k_tok = lax.broadcasted_iota(jnp.int32, (tok, TILE), 0)
                r_tok = (
                    i * (TILE // per_group)
                    + lax.broadcasted_iota(jnp.int32, (tok, TILE), 1) // per_group
                )
                s = jnp.where(k_tok <= r_tok, s, FAR)
            scores[rows, at_row] = s
            tops[back : back + 1, at_row] = jnp.max(s, axis=0, keepdims=True)
            dprob[rows, at_row] = lax.dot_general(
                vals[rows, :], do_all[at_row, :], NT, preferred_element_type=F32
            )
            return carry

        lax.fori_loop(0, tiles, step, 0, unroll=UNROLL)

    score_block(0)
    for group in groups[n_head - LAG :]:
        relay(group)
    score_block(2)
    for slot, to, there in ((1, partner, back_one), (3, at(1), back_three)):
        for group in groups:
            awaited(
                remote(
                    span.at[2, group],
                    span.at[slot, group],
                    send.at[slot, group],
                    recv.at[slot, group],
                    {"ctx": to},
                ),
                there,
            )
        score_block(slot)

    def normalise(i, carry):
        at_row = lanes_of(i)
        top = jnp.max(tops[0:SPAN, at_row], axis=0, keepdims=True)
        mass = jnp.zeros_like(top)
        moment = jnp.zeros_like(top)
        for back in range(SPAN):
            rows = rows_of(back)
            e = jnp.exp2(scores[rows, at_row] - top)
            scores[rows, at_row] = e
            mass = mass + jnp.sum(e, axis=0, keepdims=True)
            moment = moment + jnp.sum(e * dprob[rows, at_row], axis=0, keepdims=True)
        inverse = 1.0 / mass
        share[:, at_row] = inverse
        fix[:, at_row] = moment * inverse
        return carry

    lax.fori_loop(0, tiles, normalise, 0)

    def gradient_block(back):
        rows = rows_of(back)

        def step(i, carry):
            at_row = lanes_of(i)
            p = scores[rows, at_row] * share[:, at_row]
            low[rows, at_row] = p.astype(BF16)
            dsc[rows, at_row] = (p * (dprob[rows, at_row] - fix[:, at_row])).astype(BF16)
            return carry

        lax.fori_loop(0, tiles, step, 0)
        d_k = jnp.dot(dsc[rows, :], qx[:, pl.ds(0, head_dim)], preferred_element_type=F32) * inv_root
        d_v = jnp.dot(low[rows, :], do_all[...], preferred_element_type=F32)
        shape = (n_head, group_rows, head_dim)
        return d_k.reshape(shape), d_v.reshape(shape)

    def settle(back):
        for which, term in enumerate(gradient_block(back)):
            part[back - 1, :, which] = term.astype(BF16)

    @pl.when((head == 0) & ((shard == 1) | (shard == 2)))
    def _():
        pl.semaphore_wait(ready, 1)

    far_there = back_two & on_one
    near_there = (core == 0) | back_two
    for back, slot, to, there in (
        (3, 2, at(-1), back_three),
        (1, 0, partner, (core == 1) | back_two),
    ):
        settle(back)
        started(
            remote(
                part.at[slot], land.at[slot], back_send.at[slot, 0], back_recv.at[slot, 0], {"ctx": to}
            ),
            there,
        )
    settle(2)
    for slot, to, there in ((2, at(-1), far_there), (0, partner, near_there)):
        awaited(
            remote(
                part.at[slot], land.at[slot], back_send.at[slot, 0], back_recv.at[slot, 0], {"ctx": to}
            ),
            there,
        )
    on_second = (core == 1).astype(F32)
    home_order = order[::-1]
    for off in home_order:
        group = lax.rem(head + off, n_head)
        term = part[1, group].astype(F32) + land[2, group].astype(F32)
        second[group] = (term + on_second * land[0, group].astype(F32)).astype(BF16)
        started(
            remote(
                second.at[group], land.at[1, group], back_send.at[1, off], back_recv.at[1, group], {"ctx": at(-2)}
            ),
            back_two,
        )
    for which, term in enumerate(gradient_block(0)):
        own[:, which] = term

    def attended(i, carry):
        at_row = lanes_of(i)
        out = jnp.dot(valt[...], low[:, at_row], preferred_element_type=F32)
        o_ref[at_row, :] = out.T.astype(BF16)
        return carry

    lax.fori_loop(0, tiles, attended, 0)
    for off in home_order:
        group = lax.rem(head + off, n_head)
        awaited(
            remote(
                second.at[group], land.at[1, group], back_send.at[1, off], back_recv.at[1, group], {"ctx": at(-2)}
            ),
            on_two,
        )
        term = own[group] + land[1, group].astype(F32)
        term = (term + (1.0 - on_second) * land[0, group].astype(F32)).astype(BF16)
        if off:
            total[group] = term
            started(
                remote(
                    total.at[group], home.at[head], back_send.at[3, off], back_recv.at[3, head], {"head": group}
                )
            )
        else:
            home[group] = term

    def d_queries(i, carry):
        at_row = lanes_of(i)
        out = jnp.dot(keyt[...], dsc[:, at_row], preferred_element_type=F32) * inv_root
        dq_ref[at_row, :] = out.T.astype(BF16)
        return carry

    lax.fori_loop(0, tiles, d_queries, 0)
    for off in order:
        group = lax.rem(head + off, n_head)
        if off:
            awaited(
                remote(
                    total.at[group], home.at[group], back_send.at[3, off], back_recv.at[3, group], {"head": group}
                )
            )
        for which in range(2):
            wide[which, pl.ds(group, group_rows, stride=n_head), :] = home[group, which].astype(F32)
    dk_ref[...] = wide[0].astype(BF16)
    dv_ref[...] = wide[1].astype(BF16)
    for copy, when in sends:
        if when is None:
            copy.wait_send()
        else:
            pl.when(when)(copy.wait_send)


def store_kernel(*refs):
    count = (len(refs) - 1) // 2
    copies = [
        pltpu.make_async_copy(refs[i], refs[count + i], refs[-1].at[i]) for i in range(count)
    ]
    for copy in copies:
        copy.start()
    for copy in copies:
        copy.wait()


def on_device(n_ctx, n_head, queries, keys, values, grad_out, lengths):
    tok, per_group, head_dim = queries.shape
    group = keys.shape[0]
    rows = tok * per_group
    docs = lengths.shape[0]
    vmem = pl.BlockSpec(memory_space=pltpu.VMEM)
    far = pl.BlockSpec(memory_space=pltpu.HBM)
    share = (n_head, 2, group, head_dim)
    dma = pltpu.SemaphoreType.DMA
    results = (jax.ShapeDtypeStruct((rows, head_dim), BF16),) * 2 + (
        jax.ShapeDtypeStruct((group * n_head, head_dim), BF16),
    ) * 2
    kept = pl.pallas_call(
        functools.partial(fused_kernel, n_ctx, n_head),
        out_shape=results,
        in_specs=[far] * 5,
        out_specs=(vmem,) * 4,
        scratch_shapes=[
            pltpu.VMEM((rows, head_dim + docs), BF16),
            pltpu.VMEM((rows, head_dim), BF16),
            pltpu.VMEM((2, group * n_head, head_dim), BF16),
            pltpu.VMEM((2, group * n_head, head_dim), F32),
            pltpu.VMEM((1, docs), jnp.int32),
            pltpu.VMEM(share, BF16),
            pltpu.VMEM((SPAN,) + share, BF16),
            pltpu.VMEM((SPAN * tok, head_dim + docs), BF16),
            pltpu.VMEM((SPAN * tok, head_dim), BF16),
            pltpu.VMEM((head_dim, SPAN * tok), BF16),
            pltpu.VMEM((head_dim, SPAN * tok), BF16),
            pltpu.VMEM((SPAN * tok, rows), F32),
            pltpu.VMEM((SPAN * tok, rows), F32),
            pltpu.VMEM((SPAN * tok, rows), BF16),
            pltpu.VMEM((SPAN * tok, rows), BF16),
            pltpu.VMEM((8, rows), F32),
            pltpu.VMEM((1, rows), F32),
            pltpu.VMEM((1, rows), F32),
            pltpu.VMEM(share, F32),
            pltpu.VMEM((BACK,) + share, BF16),
            pltpu.VMEM((BACK,) + share, BF16),
            pltpu.VMEM(share, BF16),
            pltpu.VMEM(share, BF16),
            pltpu.VMEM(share, BF16),
            dma((5,)),
            dma((4, n_head)),
            dma((4, n_head)),
            dma((4, n_head)),
            dma((4, n_head)),
            pltpu.SemaphoreType.REGULAR,
        ],
        compiler_params=pltpu.CompilerParams(
            collective_id=0, has_side_effects=True, vmem_limit_bytes=48 << 20
        ),
    )(
        *(
            pltpu.with_memory_space_constraint(x, pltpu.HBM)
            for x in (
                queries.reshape(rows, head_dim),
                keys.reshape(-1, head_dim),
                values.reshape(-1, head_dim),
                grad_out.reshape(rows, head_dim),
                lengths.reshape(1, -1),
            )
        )
    )
    attended, d_queries, d_keys, d_values = pl.pallas_call(
        store_kernel,
        out_shape=results,
        in_specs=[vmem] * 4,
        out_specs=(far,) * 4,
        scratch_shapes=[dma((4,))],
        compiler_params=pltpu.CompilerParams(vmem_limit_bytes=4 << 20),
    )(*kept)
    return (
        attended.reshape(queries.shape),
        d_queries.reshape(queries.shape),
        d_keys.reshape(keys.shape),
        d_values.reshape(values.shape),
    )


def solution(mesh):
    rows, groups = P("ctx", "head", None), P(("ctx", "head"), None, None)
    return jax.shard_map(
        functools.partial(on_device, mesh.shape["ctx"], mesh.shape["head"]),
        mesh=mesh,
        in_specs=(rows, groups, groups, rows, P()),
        out_specs=(rows, rows, groups, groups),
        check_vma=False,
    )
```

```python
import functools
import math

import jax
import jax.numpy as jnp
from jax import lax
from jax.experimental import pallas as pl
from jax.experimental.pallas import tpu as pltpu
from jax.sharding import PartitionSpec as P

BACK = 3
SPAN = BACK + 1
LAG = 3
UNROLL = 4
TILE = 256
FAR = -1e30
MESH = pl.DeviceIdType.MESH
F32 = jnp.float32
BF16 = jnp.bfloat16
NT = (((1,), (1,)), ((), ()))


def outward(n):
    order = [0]
    for step in range(1, n // 2 + 1):
        order.append(step)
        if n - step != step:
            order.append(n - step)
    return order


def places(n_ctx):
    ctx, head = lax.axis_index("ctx"), lax.axis_index("head")
    core = lax.rem(ctx, 2)

    def at(distance):
        return jnp.clip(ctx + distance, 0, n_ctx - 1)

    return head, core, at, ctx + 1 - 2 * core


def is_first(ctx, head):
    return (ctx == 0) & (head == 0)


def greet(n_ctx, n_head, head, shard):
    barrier = pltpu.get_barrier_semaphore()
    count = jnp.int32(0)
    greets = jnp.logical_not(is_first(shard, head))
    for off in range(1, n_head):
        to = lax.rem(head + off, n_head)

        @pl.when(greets)
        def _():
            pl.semaphore_signal(barrier, inc=1, device_id={"head": to}, device_id_type=MESH)

        count = count + jnp.logical_not(is_first(shard, to)).astype(jnp.int32)
    for distance in (1, -1, 2, -2):
        there = shard + distance
        exists = (there >= 0) & (there < n_ctx)

        @pl.when(exists & greets)
        def _():
            pl.semaphore_signal(barrier, inc=1, device_id={"ctx": there}, device_id_type=MESH)

        count = count + (exists & jnp.logical_not(is_first(there, head))).astype(jnp.int32)
    return barrier, count


def remote(src, dst, send, recv, device):
    return pltpu.make_async_remote_copy(
        src_ref=src,
        dst_ref=dst,
        send_sem=send,
        recv_sem=recv,
        device_id=device,
        device_id_type=MESH,
    )


def fused_kernel(
    n_ctx,
    n_head,
    q_hbm,
    k_hbm,
    v_hbm,
    do_hbm,
    len_hbm,
    o_ref,
    dq_ref,
    dk_ref,
    dv_ref,
    qx,
    do_all,
    raw,
    wide,
    len_ref,
    mine,
    span,
    keyx,
    vals,
    keyt,
    valt,
    scores,
    dprob,
    low,
    dsc,
    tops,
    share,
    fix,
    own,
    part,
    land,
    second,
    total,
    home,
    load,
    send,
    recv,
    back_send,
    back_recv,
    ready,
):
    head, core, at, partner = places(n_ctx)
    shard = lax.axis_index("ctx")
    n_rows, head_dim = do_all.shape
    tok = keyx.shape[0] // SPAN
    per_group = n_rows // tok
    group_rows = tok // n_head
    docs = len_ref.shape[1]
    inv_root = head_dim ** (-0.5)
    expo = inv_root * math.log2(math.e)
    tiles = n_rows // TILE
    order = outward(n_head)
    near = [lax.rem(head + off, n_head) for off in order]
    spot = sum(place * (group == 0).astype(jnp.int32) for place, group in enumerate(near))
    groups = [jnp.where(place < spot, near[place], near[place + 1]) for place in range(n_head - 1)]
    groups.append(jnp.int32(0))
    sends = []
    always = None

    def started(copy, when=always):
        if when is None:
            copy.start()
        else:
            pl.when(when)(copy.start)
        sends.append((copy, when))

    def awaited(copy, when=always):
        if when is None:
            copy.wait_recv()
        else:
            pl.when(when)(copy.wait_recv)

    back_one, back_two, back_three = shard >= 1, shard >= 2, shard >= 3
    on_one, on_two = shard + 1 < n_ctx, shard + 2 < n_ctx
    barrier, greeted = greet(n_ctx, n_head, head, shard)
    k_load = pltpu.make_async_copy(k_hbm, raw.at[0], load.at[0])
    v_load = pltpu.make_async_copy(v_hbm, raw.at[1], load.at[1])
    q_load = pltpu.make_async_copy(q_hbm, qx.at[:, pl.ds(0, head_dim)], load.at[2])
    do_load = pltpu.make_async_copy(do_hbm, do_all, load.at[3])
    len_load = pltpu.make_async_copy(len_hbm, len_ref, load.at[4])
    for copy in (k_load, v_load, len_load, q_load, do_load):
        copy.start()
    k_load.wait()
    v_load.wait()
    for which in range(2):
        wide[which] = raw[which].astype(F32)
    for j in range(n_head):
        for which in range(2):
            mine[j, which] = wide[which, pl.ds(j, group_rows, stride=n_head), :].astype(BF16)
    pl.semaphore_wait(barrier, greeted)

    @pl.when(is_first(shard, head))
    def _():
        for off in range(1, n_head):
            pl.semaphore_signal(
                ready, inc=1, device_id={"head": lax.rem(head + off, n_head)}, device_id_type=MESH
            )
        for distance in (1, 2):
            pl.semaphore_signal(ready, inc=1, device_id={"ctx": at(distance)}, device_id_type=MESH)


    for off in reversed(order[1:]):
        to = lax.rem(head + off, n_head)
        started(
            remote(mine.at[to], span.at[0, head], send.at[0, off], recv.at[0, head], {"head": to}),
            jnp.logical_not(is_first(shard, to)),
        )
    started(
        remote(mine.at[head], span.at[2, head], send.at[2, head], recv.at[2, head], {"ctx": at(2)}), on_two
    )
    span[0, head] = mine[head]
    for slot, there in ((1, back_one), (2, back_two), (3, back_three)):

        @pl.when(jnp.logical_not(there))
        def _():
            span[slot] = jnp.zeros(span.shape[1:], BF16)

    for slot, missing in (
        (0, (core == 1) & (shard < 2)),
        (1, shard + 2 >= n_ctx),
        (2, (shard + 1 >= n_ctx) | (shard < 2)),
    ):

        @pl.when(missing)
        def _():
            land[slot] = jnp.zeros(land.shape[1:], BF16)

    len_load.wait()
    counts = len_ref[...].astype(F32)
    row_id = lax.broadcasted_iota(jnp.int32, (docs, docs), 0)
    lane_id = lax.broadcasted_iota(jnp.int32, (docs, docs), 1)
    column = jnp.sum(jnp.where(row_id == lane_id, counts, 0.0), axis=1, keepdims=True)
    ends = jnp.sum(jnp.where(row_id <= lane_id, column, 0.0), axis=0, keepdims=True).astype(jnp.int32)
    starts = ends - len_ref[...]
    for block in range(SPAN):
        pos = (shard - BACK + block) * tok + lax.broadcasted_iota(jnp.int32, (tok, docs), 0)
        inside = (pos >= starts) & (pos < ends)
        keyx[pl.ds(block * tok, tok), pl.ds(head_dim, docs)] = jnp.where(inside, 0.0, FAR).astype(BF16)

    def query_documents(i, carry):
        at_row = pl.ds(pl.multiple_of(i * TILE, TILE), TILE)
        q_tok = i * (TILE // per_group) + lax.broadcasted_iota(jnp.int32, (TILE, docs), 0) // per_group
        pos = shard * tok + q_tok
        inside = (pos >= starts) & (pos < ends)
        qx[at_row, pl.ds(head_dim, docs)] = jnp.where(inside, 1.0, 0.0).astype(BF16)
        return carry

    lax.fori_loop(0, tiles, query_documents, 0)

    def clear(i, carry):
        at_row = pl.ds(pl.multiple_of(i * TILE, TILE), TILE)
        for block in (0, BACK):
            keys = pl.ds(block * tok, tok)
            low[keys, at_row] = jnp.zeros((tok, TILE), BF16)
            dsc[keys, at_row] = jnp.zeros((tok, TILE), BF16)
        return carry

    lax.fori_loop(0, tiles, clear, 0)

    def relay(group):
        awaited(
            remote(
                span.at[0, group], span.at[2, group], send.at[2, group], recv.at[2, group], {"ctx": at(2)}
            ),
            back_two,
        )
        started(
            remote(
                span.at[2, group], span.at[3, group], send.at[3, group], recv.at[3, group], {"ctx": at(1)}
            ),
            back_two & on_one,
        )
        started(
            remote(
                span.at[2 * core, group],
                span.at[1, group],
                send.at[1, group],
                recv.at[1, group],
                {"ctx": partner},
            ),
            (core == 0) | back_two,
        )

    for place, group in enumerate(groups):
        other = group != head
        if place == n_head - 1:
            follows_first = (shard == 0) & (head > 0)

            @pl.when(follows_first)
            def _():
                pl.semaphore_wait(ready, 1)

            started(
                remote(
                    mine.at[0],
                    span.at[0, head],
                    send.at[0, lax.rem(n_head - head, n_head)],
                    recv.at[0, head],
                    {"head": 0},
                ),
                follows_first,
            )
        awaited(
            remote(mine.at[0], span.at[0, group], send.at[0, 0], recv.at[0, group], {"head": group}),
            other,
        )
        started(
            remote(
                span.at[0, group], span.at[2, group], send.at[2, group], recv.at[2, group], {"ctx": at(2)}
            ),
            on_two & other,
        )
        if place >= LAG:
            relay(groups[place - LAG])
    q_load.wait()
    do_load.wait()

    def rows_of(back):
        return pl.ds((BACK - back) * tok, tok)

    def needed(back, i):
        base, step = (BACK - back) * tok, TILE // per_group
        low_key = i * step if back == BACK else 0
        high_key = (i + 1) * step if back == 0 else tok
        return pl.ds(base + low_key, high_key - low_key)

    def lanes_of(i):
        return pl.ds(pl.multiple_of(i * TILE, TILE), TILE)

    def score_block(back):
        rows = rows_of(back)
        key_rows = span[back, :, 0].reshape(tok, head_dim)
        value_rows = span[back, :, 1].reshape(tok, head_dim)
        keyx[rows, pl.ds(0, head_dim)] = key_rows
        vals[rows, :] = value_rows
        keyt[:, rows] = key_rows.astype(F32).T.astype(BF16)
        valt[:, rows] = value_rows.astype(F32).T.astype(BF16)

        for i in range(tiles):
            at_row = pl.ds(i * TILE, TILE)
            keys = needed(back, i)
            s = lax.dot_general(keyx[keys, :], qx[at_row, :], NT, preferred_element_type=F32) * expo
            if back == 0:
                k_tok = lax.broadcasted_iota(jnp.int32, s.shape, 0)
                r_tok = (
                    i * (TILE // per_group) + lax.broadcasted_iota(jnp.int32, s.shape, 1) // per_group
                )
                s = jnp.where(k_tok <= r_tok, s, FAR)
            scores[keys, at_row] = s
            tops[back : back + 1, at_row] = jnp.max(s, axis=0, keepdims=True)
            dprob[keys, at_row] = lax.dot_general(
                vals[keys, :], do_all[at_row, :], NT, preferred_element_type=F32
            )

    score_block(0)
    for group in groups[n_head - LAG :]:
        relay(group)
    score_block(2)
    for slot, to, there in ((1, partner, back_one), (3, at(1), back_three)):
        for group in groups:
            awaited(
                remote(
                    span.at[2, group],
                    span.at[slot, group],
                    send.at[slot, group],
                    recv.at[slot, group],
                    {"ctx": to},
                ),
                there,
            )
        score_block(slot)

    for i in range(tiles):
        at_row = pl.ds(i * TILE, TILE)
        top = jnp.max(tops[0:SPAN, at_row], axis=0, keepdims=True)
        mass = jnp.zeros_like(top)
        moment = jnp.zeros_like(top)
        for back in range(SPAN):
            keys = needed(back, i)
            e = jnp.exp2(scores[keys, at_row] - top)
            scores[keys, at_row] = e
            mass = mass + jnp.sum(e, axis=0, keepdims=True)
            moment = moment + jnp.sum(e * dprob[keys, at_row], axis=0, keepdims=True)
        inverse = 1.0 / mass
        share[:, at_row] = inverse
        fix[:, at_row] = moment * inverse

    def weigh(keys, at_row):
        p = scores[keys, at_row] * share[:, at_row]
        low[keys, at_row] = p.astype(BF16)
        dsc[keys, at_row] = (p * (dprob[keys, at_row] - fix[:, at_row])).astype(BF16)

    def gradient_block(back):
        base, half = (BACK - back) * tok, tok // 2
        if back in (0, BACK):
            for i in range(tiles):
                weigh(needed(back, i), pl.ds(i * TILE, TILE))
            lower = pl.ds(0, n_rows) if back == 0 else pl.ds(0, n_rows // 2)
            upper = pl.ds(n_rows // 2, n_rows // 2) if back == 0 else pl.ds(0, n_rows)
            pieces = ((pl.ds(base, half), lower), (pl.ds(base + half, half), upper))
        else:

            def step(i, carry):
                weigh(rows_of(back), lanes_of(i))
                return carry

            lax.fori_loop(0, tiles, step, 0)
            pieces = ((rows_of(back), pl.ds(0, n_rows)),)
        d_k = [
            jnp.dot(dsc[keys, rows], qx[rows, pl.ds(0, head_dim)], preferred_element_type=F32)
            for keys, rows in pieces
        ]
        d_v = [
            jnp.dot(low[keys, rows], do_all[rows, :], preferred_element_type=F32)
            for keys, rows in pieces
        ]
        shape = (n_head, group_rows, head_dim)
        d_k = jnp.concatenate(d_k, axis=0) * inv_root
        return d_k.reshape(shape), jnp.concatenate(d_v, axis=0).reshape(shape)

    def settle(back):
        for which, term in enumerate(gradient_block(back)):
            part[back - 1, :, which] = term.astype(BF16)

    @pl.when((head == 0) & ((shard == 1) | (shard == 2)))
    def _():
        pl.semaphore_wait(ready, 1)

    far_there = back_two & on_one
    near_there = (core == 0) | back_two
    for back, slot, to, there in (
        (3, 2, at(-1), back_three),
        (1, 0, partner, (core == 1) | back_two),
    ):
        settle(back)
        started(
            remote(
                part.at[slot], land.at[slot], back_send.at[slot, 0], back_recv.at[slot, 0], {"ctx": to}
            ),
            there,
        )
    settle(2)
    for slot, to, there in ((2, at(-1), far_there), (0, partner, near_there)):
        awaited(
            remote(
                part.at[slot], land.at[slot], back_send.at[slot, 0], back_recv.at[slot, 0], {"ctx": to}
            ),
            there,
        )
    on_second = (core == 1).astype(F32)
    home_order = order[::-1]
    for off in home_order:
        group = lax.rem(head + off, n_head)
        term = part[1, group].astype(F32) + land[2, group].astype(F32)
        second[group] = (term + on_second * land[0, group].astype(F32)).astype(BF16)
        started(
            remote(
                second.at[group], land.at[1, group], back_send.at[1, off], back_recv.at[1, group], {"ctx": at(-2)}
            ),
            back_two,
        )
    for which, term in enumerate(gradient_block(0)):
        own[:, which] = term

    def attended(i, carry):
        at_row = lanes_of(i)
        out = jnp.dot(valt[...], low[:, at_row], preferred_element_type=F32)
        o_ref[at_row, :] = out.T.astype(BF16)
        return carry

    lax.fori_loop(0, tiles // 2, attended, 0, unroll=UNROLL)
    for off in home_order:
        group = lax.rem(head + off, n_head)
        awaited(
            remote(
                second.at[group], land.at[1, group], back_send.at[1, off], back_recv.at[1, group], {"ctx": at(-2)}
            ),
            on_two,
        )
        term = own[group] + land[1, group].astype(F32)
        term = (term + (1.0 - on_second) * land[0, group].astype(F32)).astype(BF16)
        if off:
            total[group] = term
            started(
                remote(
                    total.at[group], home.at[head], back_send.at[3, off], back_recv.at[3, head], {"head": group}
                )
            )
        else:
            home[group] = term

    def d_queries(i, carry):
        at_row = lanes_of(i)
        out = jnp.dot(keyt[...], dsc[:, at_row], preferred_element_type=F32) * inv_root
        dq_ref[at_row, :] = out.T.astype(BF16)
        return carry

    lax.fori_loop(tiles // 2, tiles, attended, 0, unroll=UNROLL)
    lax.fori_loop(0, tiles, d_queries, 0, unroll=UNROLL)
    for off in order:
        group = lax.rem(head + off, n_head)
        if off:
            awaited(
                remote(
                    total.at[group], home.at[group], back_send.at[3, off], back_recv.at[3, group], {"head": group}
                )
            )
        for which in range(2):
            wide[which, pl.ds(group, group_rows, stride=n_head), :] = home[group, which].astype(F32)
    dk_ref[...] = wide[0].astype(BF16)
    dv_ref[...] = wide[1].astype(BF16)
    for copy, when in sends:
        if when is None:
            copy.wait_send()
        else:
            pl.when(when)(copy.wait_send)


def store_kernel(*refs):
    count = (len(refs) - 1) // 2
    copies = [
        pltpu.make_async_copy(refs[i], refs[count + i], refs[-1].at[i]) for i in range(count)
    ]
    for copy in copies:
        copy.start()
    for copy in copies:
        copy.wait()


def on_device(n_ctx, n_head, queries, keys, values, grad_out, lengths):
    tok, per_group, head_dim = queries.shape
    group = keys.shape[0]
    rows = tok * per_group
    docs = lengths.shape[0]
    vmem = pl.BlockSpec(memory_space=pltpu.VMEM)
    far = pl.BlockSpec(memory_space=pltpu.HBM)
    share = (n_head, 2, group, head_dim)
    dma = pltpu.SemaphoreType.DMA
    results = (jax.ShapeDtypeStruct((rows, head_dim), BF16),) * 2 + (
        jax.ShapeDtypeStruct((group * n_head, head_dim), BF16),
    ) * 2
    kept = pl.pallas_call(
        functools.partial(fused_kernel, n_ctx, n_head),
        out_shape=results,
        in_specs=[far] * 5,
        out_specs=(vmem,) * 4,
        scratch_shapes=[
            pltpu.VMEM((rows, head_dim + docs), BF16),
            pltpu.VMEM((rows, head_dim), BF16),
            pltpu.VMEM((2, group * n_head, head_dim), BF16),
            pltpu.VMEM((2, group * n_head, head_dim), F32),
            pltpu.VMEM((1, docs), jnp.int32),
            pltpu.VMEM(share, BF16),
            pltpu.VMEM((SPAN,) + share, BF16),
            pltpu.VMEM((SPAN * tok, head_dim + docs), BF16),
            pltpu.VMEM((SPAN * tok, head_dim), BF16),
            pltpu.VMEM((head_dim, SPAN * tok), BF16),
            pltpu.VMEM((head_dim, SPAN * tok), BF16),
            pltpu.VMEM((SPAN * tok, rows), F32),
            pltpu.VMEM((SPAN * tok, rows), F32),
            pltpu.VMEM((SPAN * tok, rows), BF16),
            pltpu.VMEM((SPAN * tok, rows), BF16),
            pltpu.VMEM((8, rows), F32),
            pltpu.VMEM((1, rows), F32),
            pltpu.VMEM((1, rows), F32),
            pltpu.VMEM(share, F32),
            pltpu.VMEM((BACK,) + share, BF16),
            pltpu.VMEM((BACK,) + share, BF16),
            pltpu.VMEM(share, BF16),
            pltpu.VMEM(share, BF16),
            pltpu.VMEM(share, BF16),
            dma((5,)),
            dma((4, n_head)),
            dma((4, n_head)),
            dma((4, n_head)),
            dma((4, n_head)),
            pltpu.SemaphoreType.REGULAR,
        ],
        compiler_params=pltpu.CompilerParams(
            collective_id=0, has_side_effects=True, vmem_limit_bytes=48 << 20
        ),
    )(
        *(
            pltpu.with_memory_space_constraint(x, pltpu.HBM)
            for x in (
                queries.reshape(rows, head_dim),
                keys.reshape(-1, head_dim),
                values.reshape(-1, head_dim),
                grad_out.reshape(rows, head_dim),
                lengths.reshape(1, -1),
            )
        )
    )
    attended, d_queries, d_keys, d_values = pl.pallas_call(
        store_kernel,
        out_shape=results,
        in_specs=[vmem] * 4,
        out_specs=(far,) * 4,
        scratch_shapes=[dma((4,))],
        compiler_params=pltpu.CompilerParams(vmem_limit_bytes=4 << 20),
    )(*kept)
    return (
        attended.reshape(queries.shape),
        d_queries.reshape(queries.shape),
        d_keys.reshape(keys.shape),
        d_values.reshape(values.shape),
    )


def solution(mesh):
    rows, groups = P("ctx", "head", None), P(("ctx", "head"), None, None)
    return jax.shard_map(
        functools.partial(on_device, mesh.shape["ctx"], mesh.shape["head"]),
        mesh=mesh,
        in_specs=(rows, groups, groups, rows, P()),
        out_specs=(rows, rows, groups, groups),
        check_vma=False,
    )
```

```python
import functools
import math

import jax
import jax.numpy as jnp
from jax import lax
from jax.experimental import pallas as pl
from jax.experimental.pallas import tpu as pltpu
from jax.sharding import PartitionSpec as P

BACK = 3
SPAN = BACK + 1
LAG = 3
UNROLL = 4
TILE = 256
FAR = -1e30
MESH = pl.DeviceIdType.MESH
F32 = jnp.float32
BF16 = jnp.bfloat16
NT = (((1,), (1,)), ((), ()))


def outward(n):
    order = [0]
    for step in range(1, n // 2 + 1):
        order.append(step)
        if n - step != step:
            order.append(n - step)
    return order


def places(n_ctx):
    ctx, head = lax.axis_index("ctx"), lax.axis_index("head")
    core = lax.rem(ctx, 2)

    def at(distance):
        return jnp.clip(ctx + distance, 0, n_ctx - 1)

    return head, core, at, ctx + 1 - 2 * core


def is_first(ctx, head):
    return (ctx == 0) & (head == 0)


def greet(n_ctx, n_head, head, shard):
    barrier = pltpu.get_barrier_semaphore()
    count = jnp.int32(0)
    greets = jnp.logical_not(is_first(shard, head))
    for off in range(1, n_head):
        to = lax.rem(head + off, n_head)

        @pl.when(greets)
        def _():
            pl.semaphore_signal(barrier, inc=1, device_id={"head": to}, device_id_type=MESH)

        count = count + jnp.logical_not(is_first(shard, to)).astype(jnp.int32)
    for distance in (1, -1, 2, -2):
        there = shard + distance
        exists = (there >= 0) & (there < n_ctx)

        @pl.when(exists & greets)
        def _():
            pl.semaphore_signal(barrier, inc=1, device_id={"ctx": there}, device_id_type=MESH)

        count = count + (exists & jnp.logical_not(is_first(there, head))).astype(jnp.int32)
    return barrier, count


def remote(src, dst, send, recv, device):
    return pltpu.make_async_remote_copy(
        src_ref=src,
        dst_ref=dst,
        send_sem=send,
        recv_sem=recv,
        device_id=device,
        device_id_type=MESH,
    )


def fused_kernel(
    n_ctx,
    n_head,
    q_hbm,
    k_hbm,
    v_hbm,
    do_hbm,
    len_hbm,
    o_ref,
    dq_ref,
    dk_ref,
    dv_ref,
    qx,
    do_all,
    raw,
    wide,
    len_ref,
    mine,
    span,
    keyx,
    vals,
    keyt,
    valt,
    scores,
    dprob,
    low,
    dsc,
    tops,
    share,
    fix,
    own,
    part,
    land,
    second,
    total,
    home,
    load,
    send,
    recv,
    back_send,
    back_recv,
    ready,
):
    head, core, at, partner = places(n_ctx)
    shard = lax.axis_index("ctx")
    n_rows, head_dim = do_all.shape
    tok = keyx.shape[0] // SPAN
    per_group = n_rows // tok
    group_rows = tok // n_head
    docs = len_ref.shape[1]
    inv_root = head_dim ** (-0.5)
    expo = inv_root * math.log2(math.e)
    tiles = n_rows // TILE
    order = outward(n_head)
    near = [lax.rem(head + off, n_head) for off in order]
    spot = sum(place * (group == 0).astype(jnp.int32) for place, group in enumerate(near))
    groups = [jnp.where(place < spot, near[place], near[place + 1]) for place in range(n_head - 1)]
    groups.append(jnp.int32(0))
    sends = []
    always = None

    def started(copy, when=always):
        if when is None:
            copy.start()
        else:
            pl.when(when)(copy.start)
        sends.append((copy, when))

    def awaited(copy, when=always):
        if when is None:
            copy.wait_recv()
        else:
            pl.when(when)(copy.wait_recv)

    back_one, back_two, back_three = shard >= 1, shard >= 2, shard >= 3
    on_one, on_two = shard + 1 < n_ctx, shard + 2 < n_ctx
    barrier, greeted = greet(n_ctx, n_head, head, shard)
    k_load = pltpu.make_async_copy(k_hbm, raw.at[0], load.at[0])
    v_load = pltpu.make_async_copy(v_hbm, raw.at[1], load.at[1])
    q_load = pltpu.make_async_copy(q_hbm, qx.at[:, pl.ds(0, head_dim)], load.at[2])
    do_load = pltpu.make_async_copy(do_hbm, do_all, load.at[3])
    len_load = pltpu.make_async_copy(len_hbm, len_ref, load.at[4])
    for copy in (k_load, v_load, len_load, q_load, do_load):
        copy.start()
    k_load.wait()
    v_load.wait()
    for which in range(2):
        wide[which] = raw[which].astype(F32)
    for j in range(n_head):
        for which in range(2):
            mine[j, which] = wide[which, pl.ds(j, group_rows, stride=n_head), :].astype(BF16)
    pl.semaphore_wait(barrier, greeted)

    @pl.when(is_first(shard, head))
    def _():
        for off in range(1, n_head):
            pl.semaphore_signal(
                ready, inc=1, device_id={"head": lax.rem(head + off, n_head)}, device_id_type=MESH
            )
        for distance in (1, 2):
            pl.semaphore_signal(ready, inc=1, device_id={"ctx": at(distance)}, device_id_type=MESH)


    for off in reversed(order[1:]):
        to = lax.rem(head + off, n_head)
        started(
            remote(mine.at[to], span.at[0, head], send.at[0, off], recv.at[0, head], {"head": to}),
            jnp.logical_not(is_first(shard, to)),
        )
    started(
        remote(mine.at[head], span.at[2, head], send.at[2, head], recv.at[2, head], {"ctx": at(2)}), on_two
    )
    span[0, head] = mine[head]
    for slot, there in ((1, back_one), (2, back_two), (3, back_three)):

        @pl.when(jnp.logical_not(there))
        def _():
            span[slot] = jnp.zeros(span.shape[1:], BF16)

    for slot, missing in (
        (0, (core == 1) & (shard < 2)),
        (1, shard + 2 >= n_ctx),
        (2, (shard + 1 >= n_ctx) | (shard < 2)),
    ):

        @pl.when(missing)
        def _():
            land[slot] = jnp.zeros(land.shape[1:], BF16)

    len_load.wait()
    counts = len_ref[...].astype(F32)
    row_id = lax.broadcasted_iota(jnp.int32, (docs, docs), 0)
    lane_id = lax.broadcasted_iota(jnp.int32, (docs, docs), 1)
    column = jnp.sum(jnp.where(row_id == lane_id, counts, 0.0), axis=1, keepdims=True)
    ends = jnp.sum(jnp.where(row_id <= lane_id, column, 0.0), axis=0, keepdims=True).astype(jnp.int32)
    starts = ends - len_ref[...]
    for block in range(SPAN):
        pos = (shard - BACK + block) * tok + lax.broadcasted_iota(jnp.int32, (tok, docs), 0)
        inside = (pos >= starts) & (pos < ends)
        keyx[pl.ds(block * tok, tok), pl.ds(head_dim, docs)] = jnp.where(inside, 0.0, FAR).astype(BF16)

    def query_documents(i, carry):
        at_row = pl.ds(pl.multiple_of(i * TILE, TILE), TILE)
        q_tok = i * (TILE // per_group) + lax.broadcasted_iota(jnp.int32, (TILE, docs), 0) // per_group
        pos = shard * tok + q_tok
        inside = (pos >= starts) & (pos < ends)
        qx[at_row, pl.ds(head_dim, docs)] = jnp.where(inside, 1.0, 0.0).astype(BF16)
        return carry

    lax.fori_loop(0, tiles, query_documents, 0)

    def clear(i, carry):
        at_row = pl.ds(pl.multiple_of(i * TILE, TILE), TILE)
        for block in (0, BACK):
            keys = pl.ds(block * tok, tok)
            low[keys, at_row] = jnp.zeros((tok, TILE), BF16)
            dsc[keys, at_row] = jnp.zeros((tok, TILE), BF16)
        return carry

    lax.fori_loop(0, tiles, clear, 0)

    def relay(group):
        awaited(
            remote(
                span.at[0, group], span.at[2, group], send.at[2, group], recv.at[2, group], {"ctx": at(2)}
            ),
            back_two,
        )
        started(
            remote(
                span.at[2, group], span.at[3, group], send.at[3, group], recv.at[3, group], {"ctx": at(1)}
            ),
            back_two & on_one,
        )
        started(
            remote(
                span.at[2 * core, group],
                span.at[1, group],
                send.at[1, group],
                recv.at[1, group],
                {"ctx": partner},
            ),
            (core == 0) | back_two,
        )

    for place, group in enumerate(groups):
        other = group != head
        if place == n_head - 1:
            follows_first = (shard == 0) & (head > 0)

            @pl.when(follows_first)
            def _():
                pl.semaphore_wait(ready, 1)

            started(
                remote(
                    mine.at[0],
                    span.at[0, head],
                    send.at[0, lax.rem(n_head - head, n_head)],
                    recv.at[0, head],
                    {"head": 0},
                ),
                follows_first,
            )
        awaited(
            remote(mine.at[0], span.at[0, group], send.at[0, 0], recv.at[0, group], {"head": group}),
            other,
        )
        started(
            remote(
                span.at[0, group], span.at[2, group], send.at[2, group], recv.at[2, group], {"ctx": at(2)}
            ),
            on_two & other,
        )
        if place >= LAG:
            relay(groups[place - LAG])
    q_load.wait()
    do_load.wait()

    def rows_of(back):
        return pl.ds((BACK - back) * tok, tok)

    def needed(back, i):
        base, step = (BACK - back) * tok, TILE // per_group
        low_key = i * step if back == BACK else 0
        high_key = (i + 1) * step if back == 0 else tok
        return pl.ds(base + low_key, high_key - low_key)

    def lanes_of(i):
        return pl.ds(pl.multiple_of(i * TILE, TILE), TILE)

    def in_pieces(keys):
        return [pl.ds(keys.start + at_key, 32) for at_key in range(0, keys.size, 32)]

    def score_block(back):
        rows = rows_of(back)
        key_rows = span[back, :, 0].reshape(tok, head_dim)
        value_rows = span[back, :, 1].reshape(tok, head_dim)
        keyx[rows, pl.ds(0, head_dim)] = key_rows
        vals[rows, :] = value_rows
        keyt[:, rows] = key_rows.astype(F32).T.astype(BF16)
        valt[:, rows] = value_rows.astype(F32).T.astype(BF16)

        for i in range(tiles):
            at_row = pl.ds(i * TILE, TILE)
            keys = needed(back, i)
            s = lax.dot_general(keyx[keys, :], qx[at_row, :], NT, preferred_element_type=F32) * expo
            if back == 0:
                k_tok = lax.broadcasted_iota(jnp.int32, s.shape, 0)
                r_tok = (
                    i * (TILE // per_group) + lax.broadcasted_iota(jnp.int32, s.shape, 1) // per_group
                )
                s = jnp.where(k_tok <= r_tok, s, FAR)
            scores[keys, at_row] = s
            tops[back : back + 1, at_row] = jnp.max(s, axis=0, keepdims=True)
            dprob[keys, at_row] = lax.dot_general(
                vals[keys, :], do_all[at_row, :], NT, preferred_element_type=F32
            )

    score_block(0)
    for group in groups[n_head - LAG :]:
        relay(group)
    score_block(2)
    for slot, to, there in ((1, partner, back_one), (3, at(1), back_three)):
        for group in groups:
            awaited(
                remote(
                    span.at[2, group],
                    span.at[slot, group],
                    send.at[slot, group],
                    recv.at[slot, group],
                    {"ctx": to},
                ),
                there,
            )
        score_block(slot)

    for i in range(tiles):
        at_row = pl.ds(i * TILE, TILE)
        top = jnp.max(tops[0:SPAN, at_row], axis=0, keepdims=True)
        mass = jnp.zeros((8, TILE), F32)
        moment = jnp.zeros((8, TILE), F32)
        for back in range(SPAN):
            for keys in in_pieces(needed(back, i)):
                e = jnp.exp2(scores[keys, at_row] - top)
                scores[keys, at_row] = e
                mass = mass + jnp.sum(e.reshape(-1, 8, TILE), axis=0)
                term = e * dprob[keys, at_row]
                moment = moment + jnp.sum(term.reshape(-1, 8, TILE), axis=0)
        mass = jnp.sum(mass, axis=0, keepdims=True)
        moment = jnp.sum(moment, axis=0, keepdims=True)
        inverse = 1.0 / mass
        share[:, at_row] = inverse
        fix[:, at_row] = moment * inverse

    def weigh(keys, at_row):
        p = scores[keys, at_row] * share[:, at_row]
        low[keys, at_row] = p.astype(BF16)
        dsc[keys, at_row] = (p * (dprob[keys, at_row] - fix[:, at_row])).astype(BF16)

    def gradient_block(back):
        base, half = (BACK - back) * tok, tok // 2
        if back in (0, BACK):
            for i in range(tiles):
                for keys in in_pieces(needed(back, i)):
                    weigh(keys, pl.ds(i * TILE, TILE))
            lower = pl.ds(0, n_rows) if back == 0 else pl.ds(0, n_rows // 2)
            upper = pl.ds(n_rows // 2, n_rows // 2) if back == 0 else pl.ds(0, n_rows)
            pieces = ((pl.ds(base, half), lower), (pl.ds(base + half, half), upper))
        else:

            def step(i, carry):
                weigh(rows_of(back), lanes_of(i))
                return carry

            lax.fori_loop(0, tiles, step, 0)
            pieces = ((rows_of(back), pl.ds(0, n_rows)),)
        d_k = [
            jnp.dot(dsc[keys, rows], qx[rows, pl.ds(0, head_dim)], preferred_element_type=F32)
            for keys, rows in pieces
        ]
        d_v = [
            jnp.dot(low[keys, rows], do_all[rows, :], preferred_element_type=F32)
            for keys, rows in pieces
        ]
        shape = (n_head, group_rows, head_dim)
        d_k = jnp.concatenate(d_k, axis=0) * inv_root
        return d_k.reshape(shape), jnp.concatenate(d_v, axis=0).reshape(shape)

    def settle(back):
        for which, term in enumerate(gradient_block(back)):
            part[back - 1, :, which] = term.astype(BF16)

    @pl.when((head == 0) & ((shard == 1) | (shard == 2)))
    def _():
        pl.semaphore_wait(ready, 1)

    home_order = order[::-1]

    def piece(slot, off, to):
        group = lax.rem(head + off, n_head)
        return remote(
            part.at[slot, group],
            land.at[slot, group],
            back_send.at[slot, off],
            back_recv.at[slot, group],
            {"ctx": to},
        )

    far_there = back_two & on_one
    near_there = (core == 0) | back_two
    for back, slot, to, there in (
        (3, 2, at(-1), back_three),
        (1, 0, partner, (core == 1) | back_two),
    ):
        settle(back)
        for off in home_order:
            started(piece(slot, off, to), there)
    settle(2)
    on_second = (core == 1).astype(F32)
    for off in home_order:
        group = lax.rem(head + off, n_head)
        awaited(piece(2, off, at(-1)), far_there)
        awaited(piece(0, off, partner), near_there)
        term = part[1, group].astype(F32) + land[2, group].astype(F32)
        second[group] = (term + on_second * land[0, group].astype(F32)).astype(BF16)
        started(
            remote(
                second.at[group], land.at[1, group], back_send.at[1, off], back_recv.at[1, group], {"ctx": at(-2)}
            ),
            back_two,
        )
    for which, term in enumerate(gradient_block(0)):
        own[:, which] = term

    def attended(i, carry):
        at_row = lanes_of(i)
        out = jnp.dot(valt[...], low[:, at_row], preferred_element_type=F32)
        o_ref[at_row, :] = out.T.astype(BF16)
        return carry

    lax.fori_loop(0, tiles // 2, attended, 0, unroll=UNROLL)
    for off in home_order:
        group = lax.rem(head + off, n_head)
        awaited(
            remote(
                second.at[group], land.at[1, group], back_send.at[1, off], back_recv.at[1, group], {"ctx": at(-2)}
            ),
            on_two,
        )
        term = own[group] + land[1, group].astype(F32)
        term = (term + (1.0 - on_second) * land[0, group].astype(F32)).astype(BF16)
        if off:
            total[group] = term
            started(
                remote(
                    total.at[group], home.at[head], back_send.at[3, off], back_recv.at[3, head], {"head": group}
                )
            )
        else:
            home[group] = term

    def d_queries(i, carry):
        at_row = lanes_of(i)
        out = jnp.dot(keyt[...], dsc[:, at_row], preferred_element_type=F32) * inv_root
        dq_ref[at_row, :] = out.T.astype(BF16)
        return carry

    lax.fori_loop(tiles // 2, tiles, attended, 0, unroll=UNROLL)
    lax.fori_loop(0, tiles, d_queries, 0, unroll=UNROLL)
    for off in order:
        group = lax.rem(head + off, n_head)
        if off:
            awaited(
                remote(
                    total.at[group], home.at[group], back_send.at[3, off], back_recv.at[3, group], {"head": group}
                )
            )
        for which in range(2):
            wide[which, pl.ds(group, group_rows, stride=n_head), :] = home[group, which].astype(F32)
    dk_ref[...] = wide[0].astype(BF16)
    dv_ref[...] = wide[1].astype(BF16)
    for copy, when in sends:
        if when is None:
            copy.wait_send()
        else:
            pl.when(when)(copy.wait_send)


def store_kernel(*refs):
    count = (len(refs) - 1) // 2
    copies = [
        pltpu.make_async_copy(refs[i], refs[count + i], refs[-1].at[i]) for i in range(count)
    ]
    for copy in copies:
        copy.start()
    for copy in copies:
        copy.wait()


def on_device(n_ctx, n_head, queries, keys, values, grad_out, lengths):
    tok, per_group, head_dim = queries.shape
    group = keys.shape[0]
    rows = tok * per_group
    docs = lengths.shape[0]
    vmem = pl.BlockSpec(memory_space=pltpu.VMEM)
    far = pl.BlockSpec(memory_space=pltpu.HBM)
    share = (n_head, 2, group, head_dim)
    dma = pltpu.SemaphoreType.DMA
    results = (jax.ShapeDtypeStruct((rows, head_dim), BF16),) * 2 + (
        jax.ShapeDtypeStruct((group * n_head, head_dim), BF16),
    ) * 2
    kept = pl.pallas_call(
        functools.partial(fused_kernel, n_ctx, n_head),
        out_shape=results,
        in_specs=[far] * 5,
        out_specs=(vmem,) * 4,
        scratch_shapes=[
            pltpu.VMEM((rows, head_dim + docs), BF16),
            pltpu.VMEM((rows, head_dim), BF16),
            pltpu.VMEM((2, group * n_head, head_dim), BF16),
            pltpu.VMEM((2, group * n_head, head_dim), F32),
            pltpu.VMEM((1, docs), jnp.int32),
            pltpu.VMEM(share, BF16),
            pltpu.VMEM((SPAN,) + share, BF16),
            pltpu.VMEM((SPAN * tok, head_dim + docs), BF16),
            pltpu.VMEM((SPAN * tok, head_dim), BF16),
            pltpu.VMEM((head_dim, SPAN * tok), BF16),
            pltpu.VMEM((head_dim, SPAN * tok), BF16),
            pltpu.VMEM((SPAN * tok, rows), F32),
            pltpu.VMEM((SPAN * tok, rows), F32),
            pltpu.VMEM((SPAN * tok, rows), BF16),
            pltpu.VMEM((SPAN * tok, rows), BF16),
            pltpu.VMEM((8, rows), F32),
            pltpu.VMEM((1, rows), F32),
            pltpu.VMEM((1, rows), F32),
            pltpu.VMEM(share, F32),
            pltpu.VMEM((BACK,) + share, BF16),
            pltpu.VMEM((BACK,) + share, BF16),
            pltpu.VMEM(share, BF16),
            pltpu.VMEM(share, BF16),
            pltpu.VMEM(share, BF16),
            dma((5,)),
            dma((4, n_head)),
            dma((4, n_head)),
            dma((4, n_head)),
            dma((4, n_head)),
            pltpu.SemaphoreType.REGULAR,
        ],
        compiler_params=pltpu.CompilerParams(
            collective_id=0, has_side_effects=True, vmem_limit_bytes=48 << 20
        ),
    )(
        *(
            pltpu.with_memory_space_constraint(x, pltpu.HBM)
            for x in (
                queries.reshape(rows, head_dim),
                keys.reshape(-1, head_dim),
                values.reshape(-1, head_dim),
                grad_out.reshape(rows, head_dim),
                lengths.reshape(1, -1),
            )
        )
    )
    attended, d_queries, d_keys, d_values = pl.pallas_call(
        store_kernel,
        out_shape=results,
        in_specs=[vmem] * 4,
        out_specs=(far,) * 4,
        scratch_shapes=[dma((4,))],
        compiler_params=pltpu.CompilerParams(vmem_limit_bytes=4 << 20),
    )(*kept)
    return (
        attended.reshape(queries.shape),
        d_queries.reshape(queries.shape),
        d_keys.reshape(keys.shape),
        d_values.reshape(values.shape),
    )


def solution(mesh):
    rows, groups = P("ctx", "head", None), P(("ctx", "head"), None, None)
    return jax.shard_map(
        functools.partial(on_device, mesh.shape["ctx"], mesh.shape["head"]),
        mesh=mesh,
        in_specs=(rows, groups, groups, rows, P()),
        out_specs=(rows, rows, groups, groups),
        check_vma=False,
    )
```
